512 devices in a mesh: ctx: 64 (over z, x_hi, core), head: 8 (over x_lo, y).
Axes of the slice: x: 4 (x_hi: 2, x_lo: 2; x = x_hi * 2 + x_lo), y: 4, z: 16, core: 2. Of those that a mesh axis runs over, the one named last changes fastest.
Arguments:
- queries: bfloat16 [16384, 4096], P('ctx', 'head'), may hold values from -6 to 6
- key_rows: bfloat16 [16384, 1024], P('ctx', 'head'), may hold values from -6 to 6
- value_rows: bfloat16 [16384, 1024], P('ctx', 'head'), may hold values from -6 to 6
- attn_out: bfloat16 [16384, 4096], P('ctx', 'head'), may hold values from -6 to 6
- out_grad: bfloat16 [16384, 4096], P('ctx', 'head'), may hold values from -6 to 6
- log_sums: float32 [32, 16384], P('head', 'ctx'), may hold values from 4.5 to 6
- block_picks: int32 [128, 32, 3], P('ctx', 'head'), may hold values from 0 to 3, all different within a row
- query_weight: bfloat16 [4096, 4096], P('ctx', 'head'), may hold values from -0.21875 to 0.21875
- key_weight: bfloat16 [4096, 1024], P('ctx', 'head'), may hold values from -0.21875 to 0.21875
- value_weight: bfloat16 [4096, 1024], P('ctx', 'head'), may hold values from -0.21875 to 0.21875
Outputs:
- input_grad: bfloat16 [16384, 4096], P('ctx', 'head')
The draws below stay inside these ranges and needn't reach their ends.
Inputs may be any that keep to these rules, and one draw needn't show every extreme that they name: `block_picks`: in each row (query block, query head) the 3 entries differ; entry m selects the block m + 1 blocks before the query's block, and selections before the sequence's start select nothing.
All inputs are finite; a program needn't handle non-finite values.
Results may differ from the reference program's by a relative error of at most 0.013.
Values may be sent and summed in bfloat16 or wider, within the bound.
No kernel may reach another device: no remote copies, remote signals or barrier semaphores. Data moves between devices by JAX's collectives and lax.ppermute only.
A program may use at most 64 MiB of HBM per device.

```python
import math
import jax
import jax.numpy as jnp
from jax import lax

D = 4096
HD = 128
GROUP = 4
BLK = 128
TOPK = 3
KV_HEADS = 8
QHEADS = 32
TOKENS = 16384
NQB = 128
WINDOW = 4


def steps_of(own_key, dims, split, least, high):
    def one(axis_at, shards_of):
        heights = jax.random.uniform(jax.random.fold_in(jax.random.fold_in(own_key, 6), axis_at), (shards_of,), jnp.float32, least / len(split), high / len(split))
        return jnp.repeat(jnp.exp(heights), dims[axis_at] // shards_of).reshape((-1,) + (1,) * (len(dims) - axis_at - 1))

    level = one(*split[0])
    for cut in split[1:]:
        level = level * one(*cut)
    return level


def picks_of(own_key, rows, amount, top, lift):
    order = jax.random.permutation(jax.random.fold_in(own_key, 1), amount)
    pull = order
    for power in range(3):
        pull = pull * pull // amount
    pull = pull * lift // amount
    lots = jax.random.randint(jax.random.fold_in(own_key, 2), (rows, amount), 0, 4096) + pull
    holders = jax.random.permutation(jax.random.fold_in(own_key, 3), rows)[jnp.arange(amount) % rows]
    lots = jnp.where(jnp.arange(rows)[:, None] == holders[None, :], 1 << 14, lots)
    score = lots * amount + jnp.arange(amount)
    return lax.top_k(score.astype(jnp.int32), top)[1].astype(jnp.int32)


def noise(rng, shape, spread, most, shards=(), kind=jnp.bfloat16):
    drawn = spread * jax.random.normal(rng, shape, jnp.float32)
    if shards:
        drawn = drawn * steps_of(rng, shape, shards, -0.22, 0.18)
    return jnp.clip(drawn, -most, most).astype(kind)


def setup_inputs(seed: int = 0) -> dict:
    key_of = jax.random.split(jax.random.key(seed), 11)
    queries = noise(key_of[0], (TOKENS, QHEADS * HD), 1.0, 6.0, ((0, 64), (1, 8)))
    key_rows = noise(key_of[1], (TOKENS, KV_HEADS * HD), 1.0, 6.0, ((0, 64), (1, 8)))
    value_rows = noise(key_of[2], (TOKENS, KV_HEADS * HD), 1.0, 6.0, ((0, 64), (1, 8)))
    attn_out = noise(key_of[3], (TOKENS, QHEADS * HD), 1.0, 6.0, ((0, 64), (1, 8)))
    out_grad = noise(key_of[4], (TOKENS, QHEADS * HD), 1.0, 6.0, ((0, 64), (1, 8)))
    log_sums = jnp.clip(4.5 + 1.5 * jax.random.uniform(key_of[5], (QHEADS, TOKENS), jnp.float32) ** steps_of(key_of[5], (QHEADS, TOKENS), ((0, 8), (1, 64)), -0.2, 0.2), 4.5, 6.0)
    block_picks = picks_of(key_of[6], NQB * QHEADS, WINDOW, TOPK, 6144).reshape((NQB, QHEADS, TOPK))
    query_weight = noise(key_of[7], (D, QHEADS * HD), ((GROUP + 2) * HD) ** -0.5, 0.21875, ((0, 64), (1, 8)))
    key_weight = noise(key_of[8], (D, KV_HEADS * HD), ((GROUP + 2) * HD) ** -0.5, 0.21875, ((0, 64), (1, 8)))
    value_weight = noise(key_of[9], (D, KV_HEADS * HD), ((GROUP + 2) * HD) ** -0.5, 0.21875, ((0, 64), (1, 8)))
    return dict(queries=queries, key_rows=key_rows, value_rows=value_rows, attn_out=attn_out, out_grad=out_grad, log_sums=log_sums, block_picks=block_picks, query_weight=query_weight, key_weight=key_weight, value_weight=value_weight)


def rounded(values_in):
    return lax.optimization_barrier(values_in.astype(jnp.bfloat16)).astype(jnp.float32)

def head_grads(query_part, grad_part, log_part, delta_part, pick_part, key_table, value_table):
    blocks, width, group, head_dim = query_part.shape
    scaling = 1.0 / math.sqrt(head_dim)
    offsets = jnp.concatenate([jnp.zeros((blocks, group, 1), jnp.int32), pick_part.astype(jnp.int32) + 1], axis=2)
    key_block = jnp.arange(blocks, dtype=jnp.int32)[:, None, None] - offsets
    usable = key_block >= 0
    clipped = jnp.clip(key_block, 0, blocks - 1).astype(jnp.int32)
    key_sel = key_table[clipped]
    value_sel = value_table[clipped]
    scores = jnp.einsum('bqgd,bgskd->bgqsk', query_part, key_sel) * scaling
    position = jnp.arange(width)
    causal = position[:, None] >= position[None, :]
    allowed = usable[:, :, None, :, None] & ((offsets != 0)[:, :, None, :, None] | causal[None, None, :, None, :])
    probability = jnp.where(allowed, jnp.exp(scores - log_part[:, :, :, None, None]), 0.0)
    prob_grad = jnp.einsum('bqgd,bgskd->bgqsk', grad_part, value_sel)
    score_grad = probability * (prob_grad - delta_part[:, :, :, None, None])
    prob_half = rounded(probability)
    grad_half = rounded(score_grad)
    query_grad = jnp.einsum('bgqsk,bgskd->bqgd', grad_half, key_sel) * scaling
    key_terms = jnp.einsum('bgqsk,bqgd->bgskd', grad_half, query_part) * scaling
    value_terms = jnp.einsum('bgqsk,bqgd->bgskd', prob_half, grad_part)
    flat_index = clipped.reshape(-1)
    key_grad = jax.ops.segment_sum(key_terms.reshape(-1, width, head_dim), flat_index, num_segments=blocks)
    value_grad = jax.ops.segment_sum(value_terms.reshape(-1, width, head_dim), flat_index, num_segments=blocks)
    return (query_grad, key_grad, value_grad)

def reference(queries, key_rows, value_rows, attn_out, out_grad, log_sums, block_picks, query_weight, key_weight, value_weight):
    blocks = TOKENS // BLK
    stacked = (queries.reshape(blocks, BLK, KV_HEADS, GROUP, HD).transpose(2, 0, 1, 3, 4), out_grad.reshape(blocks, BLK, KV_HEADS, GROUP, HD).transpose(2, 0, 1, 3, 4), attn_out.reshape(blocks, BLK, KV_HEADS, GROUP, HD).transpose(2, 0, 1, 3, 4), key_rows.reshape(blocks, BLK, KV_HEADS, HD).transpose(2, 0, 1, 3), value_rows.reshape(blocks, BLK, KV_HEADS, HD).transpose(2, 0, 1, 3), log_sums.reshape(KV_HEADS, GROUP, blocks, BLK).transpose(0, 2, 1, 3), block_picks.reshape(blocks, KV_HEADS, GROUP, TOPK).transpose(1, 0, 2, 3), query_weight.reshape(D, KV_HEADS, GROUP * HD).transpose(1, 0, 2), key_weight.reshape(D, KV_HEADS, HD).transpose(1, 0, 2), value_weight.reshape(D, KV_HEADS, HD).transpose(1, 0, 2))

    def step_head(total, items):
        query_part, grad_part, out_part, key_part, value_part, log_part, pick_part, query_proj, key_proj, value_proj = items
        query_full = query_part.astype(jnp.float32)
        grad_full = grad_part.astype(jnp.float32)
        delta_part = lax.optimization_barrier(jnp.sum(grad_full * out_part.astype(jnp.float32), axis=3)).transpose(0, 2, 1)
        query_grad, key_grad, value_grad = head_grads(query_full, grad_full, log_part, delta_part, pick_part, key_part.astype(jnp.float32), value_part.astype(jnp.float32))
        grads = jnp.concatenate([query_grad.reshape(TOKENS, GROUP * HD).astype(jnp.bfloat16), key_grad.reshape(TOKENS, HD).astype(jnp.bfloat16), value_grad.reshape(TOKENS, HD).astype(jnp.bfloat16)], axis=1)
        weight_cat = jnp.concatenate([query_proj, key_proj, value_proj], axis=1)
        partial_value = jnp.dot(grads, weight_cat.T, preferred_element_type=jnp.float32)
        return (total + rounded(partial_value), None)
    total, unused = lax.scan(step_head, jnp.zeros((TOKENS, D), jnp.float32), stacked)
    return total.astype(jnp.bfloat16)
```

```python
import math

import jax
import jax.numpy as jnp
from jax import lax
from jax.experimental import pallas as pl
from jax.experimental.pallas import tpu as pltpu
from jax.sharding import Mesh
from jax.sharding import PartitionSpec as P


BLK = 128
HD = 128
GROUP = 4
BF = jnp.bfloat16
F32 = jnp.float32
Z = ("zh", "zl")
CTX = ("zh", "zl", "xh", "core")
HEAD = ("xl", "y")
NT = (((1,), (1,)), ((), ()))
NN = (((1,), (0,)), ((), ()))
TN = (((0,), (0,)), ((), ()))


def dot(a, b, dims):
    return lax.dot_general(a, b, dims, preferred_element_type=F32)


def passed_along(x, axis, by):
    n = lax.axis_size(axis)
    pairs = [(i, i + by) for i in range(n) if 0 <= i + by < n]
    return lax.ppermute(x, axis, pairs)


def shifted(x, axis, by):
    n = lax.axis_size(axis)
    return lax.ppermute(x, axis, [(i, (i + by) % n) for i in range(n)])


def attention_kernel(
    where_ref, picks_ref, q_ref, do_ref, o_ref, lse_ref, kv0_ref, kv1_ref, kv2_ref,
    aq_ref, own_ref, ret1_ref, ret2_ref,
):
    scaling = 1.0 / math.sqrt(HD)
    first = where_ref[0] * 2
    tables = (kv2_ref, kv2_ref, kv1_ref, kv1_ref, kv0_ref, kv0_ref)
    sums = (ret2_ref, ret2_ref, ret1_ref, ret1_ref, own_ref, own_ref)
    key_at = lax.broadcasted_iota(jnp.int32, (BLK, BLK), 0)
    query_at = lax.broadcasted_iota(jnp.int32, (BLK, BLK), 1)
    causal = key_at <= query_at
    dk = [None] * 6
    dv = [None] * 6
    for b in range(2):
        rows = slice(BLK * b, BLK * b + BLK)
        cols = [slice(HD * h, HD * h + HD) for h in range(GROUP)]
        q = jnp.concatenate([q_ref[rows, c] for c in cols], axis=0)
        do = jnp.concatenate([do_ref[rows, c] for c in cols], axis=0)
        lse = []
        delta = []
        for h in range(GROUP):
            prod = do_ref[rows, cols[h]].astype(F32) * o_ref[rows, cols[h]].astype(F32)
            delta.append(jnp.sum(prod.T, axis=0, keepdims=True))
            lse.append(lse_ref[h : h + 1, rows])
        dq = None
        for s in range(5):
            c = b + s
            half = slice(BLK * (c % 2), BLK * (c % 2) + BLK)
            k = tables[c][half, :HD]
            v = tables[c][half, HD:]
            scores = dot(k, q, NT)
            prob_grad = dot(v, do, NT)
            p_parts = []
            g_parts = []
            for h in range(GROUP):
                at = slice(BLK * h, BLK * h + BLK)
                p = jnp.exp(scores[:, at] * scaling - lse[h])
                if s == 4:
                    p = jnp.where(causal, p, 0.0)
                else:
                    m = 3 - s
                    used = picks_ref[b, h, 0] == m
                    for t in range(1, 3):
                        used = used | (picks_ref[b, h, t] == m)
                    used = used & (first + b - 1 - m >= 0)
                    p = jnp.where(used, p, 0.0)
                p_parts.append(p.astype(BF))
                g_parts.append((p * (prob_grad[:, at] - delta[h])).astype(BF))
            p_half = jnp.concatenate(p_parts, axis=1)
            g_half = jnp.concatenate(g_parts, axis=1)
            part = dot(g_half, k, TN)
            dq = part if dq is None else dq + part
            k_part = dot(g_half, q, NN)
            v_part = dot(p_half, do, NN)
            dk[c] = k_part if dk[c] is None else dk[c] + k_part
            dv[c] = v_part if dv[c] is None else dv[c] + v_part
        for h in range(GROUP):
            aq_ref[rows, cols[h]] = (dq[BLK * h : BLK * h + BLK] * scaling).astype(BF)
    for c in range(6):
        half = slice(BLK * (c % 2), BLK * (c % 2) + BLK)
        sums[c][half, :HD] = (dk[c] * scaling).astype(sums[c].dtype)
        sums[c][half, HD:] = dv[c].astype(sums[c].dtype)


def attention(where, picks, q, do, o, lse, kv0, kv1, kv2):
    tokens = q.shape[0]
    vm = pl.BlockSpec(memory_space=pltpu.VMEM)
    sm = pl.BlockSpec(memory_space=pltpu.SMEM)
    return pl.pallas_call(
        attention_kernel,
        out_shape=(
            jax.ShapeDtypeStruct(q.shape, BF),
            jax.ShapeDtypeStruct((tokens, 2 * HD), F32),
            jax.ShapeDtypeStruct((tokens, 2 * HD), BF),
            jax.ShapeDtypeStruct((tokens, 2 * HD), BF),
        ),
        in_specs=[sm, sm] + [vm] * 7,
        out_specs=(vm,) * 4,
        name="attention",
    )(where, picks, q, do, o, lse, kv0, kv1, kv2)


def project_kernel(where_ref, aq_ref, akv_ref, wc_ref, wo_ref, out_ref):
    zl = where_ref[1]
    core = where_ref[2]
    for head in range(8):
        zh = head // 2
        wide = []
        for e in range(2):
            k = lax.rem(2 * (head % 2) + e + 4 - zl, 4)
            mine = wc_ref[k, zh]
            other = wo_ref[k, zh]
            wide.append(jnp.where(core == 0, mine, other))
            wide.append(jnp.where(core == 0, other, mine))
        w = jnp.concatenate(wide, axis=0)
        for r in range(2):
            total = dot(aq_ref[r], w[:, : GROUP * HD], NT) + dot(akv_ref[r], w[:, GROUP * HD :], NT)
            out_ref[8 * r + head] = total.astype(BF)


def project(where, aq, akv, wc, wo):
    vm = pl.BlockSpec(memory_space=pltpu.VMEM)
    return pl.pallas_call(
        project_kernel,
        out_shape=jax.ShapeDtypeStruct((16, aq.shape[1], 256), BF),
        in_specs=[pl.BlockSpec(memory_space=pltpu.SMEM)] + [vm] * 4,
        out_specs=vm,
        name="project",
    )(where, aq, akv, wc, wo)


def total_kernel(in_ref, out_ref):
    for xh in range(2):
        total = in_ref[8 * xh].astype(F32)
        for h in range(1, 8):
            total = total + in_ref[8 * xh + h].astype(F32)
        for e in range(2):
            at = 256 * e + 128 * xh
            out_ref[:, at : at + 128] = total[:, 128 * e : 128 * e + 128].astype(BF)


def totalled(parts):
    rows = parts.shape[1]
    step = 64
    return pl.pallas_call(
        total_kernel,
        grid=(rows // step,),
        out_shape=jax.ShapeDtypeStruct((rows, 512), BF),
        in_specs=[pl.BlockSpec((16, step, 256), lambda i: (0, i, 0))],
        out_specs=pl.BlockSpec((step, 512), lambda i: (i, 0)),
        name="total",
    )(parts)


def per_device(
    queries, key_rows, value_rows, attn_out, out_grad, log_sums, block_picks,
    query_weight, key_weight, value_weight,
):
    where = jnp.stack(
        [lax.axis_index(CTX), lax.axis_index("zl"), lax.axis_index("core")]
    ).astype(jnp.int32)
    kv0 = jnp.concatenate([key_rows, value_rows], axis=1)
    kv1 = passed_along(kv0, CTX, 1)
    kv2 = passed_along(kv0, CTX, 2)
    weight = jnp.concatenate([query_weight, key_weight, value_weight], axis=1)
    w0 = lax.all_gather(weight, "zh")
    w1 = shifted(w0, Z, -1)
    w3 = shifted(w0, Z, 1)
    w2a = shifted(w0[:2], Z, -2)
    w2b = shifted(w0[2:], Z, 2)
    aq, own, ret1, ret2 = attention(
        where, block_picks, queries, out_grad, attn_out, log_sums, kv0, kv1, kv2
    )
    back1 = passed_along(ret1, CTX, -1)
    back2 = passed_along(ret2, CTX, -2)
    aq_all = lax.all_gather(aq, "xh")
    akv = (own + back1.astype(F32) + back2.astype(F32)).astype(BF)
    akv_all = lax.all_gather(akv, "xh")
    wc = jnp.concatenate([w0, w1, w2a, w2b, w3], axis=0).reshape(4, 4, *weight.shape)
    wo = shifted(wc, "core", 1)
    parts = project(where, aq_all, akv_all, wc, wo)
    parts = lax.all_to_all(parts, ("xh", "xl", "y"), 0, 0)
    return totalled(parts)


def solution(mesh):
    wide = Mesh(
        mesh.devices.reshape(4, 4, 2, 2, 2, 4), ("zh", "zl", "xh", "core", "xl", "y")
    )
    both = P(CTX, HEAD)
    placed = (both,) * 5 + (P(HEAD, CTX), P(CTX, HEAD, None)) + (both,) * 3
    return jax.shard_map(
        per_device, mesh=wide, in_specs=placed, out_specs=both, check_vma=False
    )
```

```python
import math

import jax
import jax.numpy as jnp
from jax import lax
from jax.experimental import pallas as pl
from jax.experimental.pallas import tpu as pltpu
from jax.sharding import Mesh
from jax.sharding import PartitionSpec as P


BLK = 128
HD = 128
GROUP = 4
BF = jnp.bfloat16
F32 = jnp.float32
Z = ("zh", "zl")
CTX = ("zh", "zl", "xh", "core")
HEAD = ("xl", "y")
NT = (((1,), (1,)), ((), ()))
NN = (((1,), (0,)), ((), ()))
TN = (((0,), (0,)), ((), ()))


def dot(a, b, dims):
    return lax.dot_general(a, b, dims, preferred_element_type=F32)


def passed_along(x, axis, by):
    n = lax.axis_size(axis)
    pairs = [(i, i + by) for i in range(n) if 0 <= i + by < n]
    return lax.ppermute(x, axis, pairs)


def shifted(x, axis, by):
    n = lax.axis_size(axis)
    return lax.ppermute(x, axis, [(i, (i + by) % n) for i in range(n)])


def attention_kernel(
    picks_ref, q_ref, do_ref, o_ref, lse_ref, kv0_ref, kv1_ref, kv2_ref,
    aq_ref, own_ref, ret1_ref, ret2_ref,
):
    scaling = 1.0 / math.sqrt(HD)
    first = lax.axis_index(CTX) * 2
    tables = (kv2_ref, kv2_ref, kv1_ref, kv1_ref, kv0_ref, kv0_ref)
    sums = (ret2_ref, ret2_ref, ret1_ref, ret1_ref, own_ref, own_ref)
    key_at = lax.broadcasted_iota(jnp.int32, (BLK, BLK), 0)
    query_at = lax.broadcasted_iota(jnp.int32, (BLK, BLK), 1)
    causal = key_at <= query_at
    dk = [None] * 6
    dv = [None] * 6
    for b in range(2):
        rows = slice(BLK * b, BLK * b + BLK)
        cols = [slice(HD * h, HD * h + HD) for h in range(GROUP)]
        q = jnp.concatenate([q_ref[rows, c] for c in cols], axis=0)
        do = jnp.concatenate([do_ref[rows, c] for c in cols], axis=0)
        lse = []
        delta = []
        for h in range(GROUP):
            prod = do_ref[rows, cols[h]].astype(F32) * o_ref[rows, cols[h]].astype(F32)
            delta.append(jnp.sum(prod.T, axis=0, keepdims=True))
            lse.append(lse_ref[h : h + 1, rows])
        dq = None
        for s in range(5):
            c = b + s
            half = slice(BLK * (c % 2), BLK * (c % 2) + BLK)
            k = tables[c][half, :HD]
            v = tables[c][half, HD:]
            scores = dot(k, q, NT)
            prob_grad = dot(v, do, NT)
            p_parts = []
            g_parts = []
            for h in range(GROUP):
                at = slice(BLK * h, BLK * h + BLK)
                p = jnp.exp(scores[:, at] * scaling - lse[h])
                if s == 4:
                    p = jnp.where(causal, p, 0.0)
                else:
                    m = 3 - s
                    used = picks_ref[0, b, h] == m
                    for t in range(1, 3):
                        used = used | (picks_ref[t, b, h] == m)
                    used = used & (first + b - 1 - m >= 0)
                    p = jnp.where(used, p, 0.0)
                p_parts.append(p.astype(BF))
                g_parts.append((p * (prob_grad[:, at] - delta[h])).astype(BF))
            p_half = jnp.concatenate(p_parts, axis=1)
            g_half = jnp.concatenate(g_parts, axis=1)
            part = dot(g_half, k, TN)
            dq = part if dq is None else dq + part
            k_part = dot(g_half, q, NN)
            v_part = dot(p_half, do, NN)
            dk[c] = k_part if dk[c] is None else dk[c] + k_part
            dv[c] = v_part if dv[c] is None else dv[c] + v_part
        for h in range(GROUP):
            aq_ref[rows, cols[h]] = (dq[BLK * h : BLK * h + BLK] * scaling).astype(BF)
    for c in range(6):
        half = slice(BLK * (c % 2), BLK * (c % 2) + BLK)
        sums[c][half, :HD] = (dk[c] * scaling).astype(sums[c].dtype)
        sums[c][half, HD:] = dv[c].astype(sums[c].dtype)


def attention(picks, q, do, o, lse, kv0, kv1, kv2):
    tokens = q.shape[0]
    vm = pl.BlockSpec(memory_space=pltpu.VMEM)
    sm = pl.BlockSpec(memory_space=pltpu.SMEM)
    return pl.pallas_call(
        attention_kernel,
        out_shape=(
            jax.ShapeDtypeStruct(q.shape, BF),
            jax.ShapeDtypeStruct((tokens, 2 * HD), F32),
            jax.ShapeDtypeStruct((tokens, 2 * HD), BF),
            jax.ShapeDtypeStruct((tokens, 2 * HD), BF),
        ),
        in_specs=[sm] + [vm] * 7,
        out_specs=(vm,) * 4,
        name="attention",
    )(picks.transpose(2, 0, 1), q, do, o, lse, kv0, kv1, kv2)


def project_kernel(zl_ref, a_ref, m0_ref, o0_ref, m1_ref, o1_ref, out_ref):
    w = jnp.concatenate([r[0, 0] for r in (m0_ref, o0_ref, m1_ref, o1_ref)], axis=0)
    for r in range(2):
        out_ref[r, 0] = dot(a_ref[r], w, NT).astype(BF)


def project(zl, a, wc, wo):
    rows = wc.shape[2]

    def rows_of(e):
        def at(head, zl_ref):
            return (lax.rem(2 * lax.rem(head, 2) + e + 4 - zl_ref[0], 4), lax.div(head, 2), 0, 0)

        return pl.BlockSpec((1, 1, rows, wc.shape[3]), at)

    def whole(x):
        return pl.BlockSpec(x.shape, lambda head, zl_ref: (0, 0, 0))

    return pl.pallas_call(
        project_kernel,
        grid_spec=pltpu.PrefetchScalarGridSpec(
            num_scalar_prefetch=1,
            grid=(8,),
            in_specs=[whole(a), rows_of(0), rows_of(0), rows_of(1), rows_of(1)],
            out_specs=pl.BlockSpec(
                (2, 1, a.shape[1], 4 * rows), lambda head, zl_ref: (0, head, 0, 0)
            ),
        ),
        out_shape=jax.ShapeDtypeStruct((2, 8, a.shape[1], 4 * rows), BF),
        name="project",
    )(zl, a, wc, wo, wc, wo)


def total_kernel(in_ref, out_ref):
    swapped = lax.axis_index("core") == 1
    for xh in range(2):
        total = in_ref[8 * xh].astype(F32)
        for h in range(1, 8):
            total = total + in_ref[8 * xh + h].astype(F32)
        for e in range(2):
            at = 256 * e + 128 * xh
            tile = total[:, 128 * e : 128 * e + 128]
            tile = jnp.where(swapped, pltpu.roll(tile, 64, 1), tile)
            out_ref[:, at : at + 128] = tile.astype(BF)


def totalled(parts):
    rows = parts.shape[1]
    step = 64
    return pl.pallas_call(
        total_kernel,
        grid=(rows // step,),
        out_shape=jax.ShapeDtypeStruct((rows, 512), BF),
        in_specs=[pl.BlockSpec((16, step, 256), lambda i: (0, i, 0))],
        out_specs=pl.BlockSpec((step, 512), lambda i: (i, 0)),
        name="total",
    )(parts)


def prepare_kernel(k_ref, v_ref, qw_ref, kw_ref, vw_ref, kv_ref, w_ref):
    kv_ref[:, :HD] = k_ref[...]
    kv_ref[:, HD:] = v_ref[...]
    w_ref[:, : GROUP * HD] = qw_ref[...]
    w_ref[:, GROUP * HD : GROUP * HD + HD] = kw_ref[...]
    w_ref[:, GROUP * HD + HD :] = vw_ref[...]


def prepared(keys, values, qw, kw, vw):
    vm = pl.BlockSpec(memory_space=pltpu.VMEM)
    return pl.pallas_call(
        prepare_kernel,
        out_shape=(
            jax.ShapeDtypeStruct((keys.shape[0], 2 * HD), BF),
            jax.ShapeDtypeStruct((qw.shape[0], qw.shape[1] + 2 * HD), BF),
        ),
        in_specs=[vm] * 5,
        out_specs=(vm, vm),
        name="prepare",
    )(keys, values, qw, kw, vw)


def per_device(
    queries, key_rows, value_rows, attn_out, out_grad, log_sums, block_picks,
    query_weight, key_weight, value_weight,
):
    kv0, weight = prepared(key_rows, value_rows, query_weight, key_weight, value_weight)
    kv1 = passed_along(kv0, CTX, 1)
    kv2 = passed_along(kv0, CTX, 2)
    w0 = lax.all_gather(weight, "zh")
    w1 = shifted(w0, Z, -1)
    w3 = shifted(w0, Z, 1)
    w2 = lax.ppermute(w0, Z, [((z + 2 if z % 2 == 0 else z - 2) % 16, z) for z in range(16)])
    aq, own, ret1, ret2 = attention(
        block_picks, queries, out_grad, attn_out, log_sums, kv0, kv1, kv2
    )
    back1 = passed_along(ret1, CTX, -1)
    back2 = passed_along(ret2, CTX, -2)
    wc = jnp.stack([w0, w1, w2, w3])
    wo = shifted(wc, "core", 1)
    akv = (own + back1.astype(F32) + back2.astype(F32)).astype(BF)
    a_all = lax.all_gather(jnp.concatenate([aq, akv], axis=1), "xh")
    zl = lax.axis_index("zl").reshape(1).astype(jnp.int32)
    parts = project(zl, a_all, wc, wo)
    parts = lax.all_to_all(parts.reshape(16, *parts.shape[2:]), ("xh", "xl", "y"), 0, 0)
    return totalled(parts)


def solution(mesh):
    wide = Mesh(
        mesh.devices.reshape(4, 4, 2, 2, 2, 4), ("zh", "zl", "xh", "core", "xl", "y")
    )
    both = P(CTX, HEAD)
    placed = (both,) * 5 + (P(HEAD, CTX), P(CTX, HEAD, None)) + (both,) * 3
    return jax.shard_map(
        per_device, mesh=wide, in_specs=placed, out_specs=both, check_vma=False
    )
```

```python
import math

import jax
import jax.numpy as jnp
from jax import lax
from jax.experimental import pallas as pl
from jax.experimental.pallas import tpu as pltpu
from jax.sharding import Mesh
from jax.sharding import PartitionSpec as P


BLK = 128
HD = 128
GROUP = 4
BF = jnp.bfloat16
F32 = jnp.float32
Z = ("zh", "zl")
CTX = ("zh", "zl", "xh", "core")
HEAD = ("xl", "y")
NT = (((1,), (1,)), ((), ()))
NN = (((1,), (0,)), ((), ()))
TN = (((0,), (0,)), ((), ()))


def dot(a, b, dims):
    return lax.dot_general(a, b, dims, preferred_element_type=F32)


def passed_along(x, axis, by):
    n = lax.axis_size(axis)
    pairs = [(i, i + by) for i in range(n) if 0 <= i + by < n]
    return lax.ppermute(x, axis, pairs)


def shifted(x, axis, by):
    n = lax.axis_size(axis)
    return lax.ppermute(x, axis, [(i, (i + by) % n) for i in range(n)])


def attention_kernel(
    picks_ref, q_ref, do_ref, o_ref, lse_ref, kv0_ref, kv1_ref, kv2_ref,
    aq_ref, own_ref, ret1_ref, ret2_ref,
):
    scaling = 1.0 / math.sqrt(HD)
    first = lax.axis_index(CTX) * 2
    tables = (kv2_ref, kv2_ref, kv1_ref, kv1_ref, kv0_ref, kv0_ref)
    sums = (ret2_ref, ret2_ref, ret1_ref, ret1_ref, own_ref, own_ref)
    key_at = lax.broadcasted_iota(jnp.int32, (BLK, BLK), 0)
    query_at = lax.broadcasted_iota(jnp.int32, (BLK, BLK), 1)
    causal = key_at <= query_at
    dk = [None] * 6
    dv = [None] * 6
    for b in range(2):
        rows = slice(BLK * b, BLK * b + BLK)
        cols = [slice(HD * h, HD * h + HD) for h in range(GROUP)]
        q = jnp.concatenate([q_ref[rows, c] for c in cols], axis=0)
        do = jnp.concatenate([do_ref[rows, c] for c in cols], axis=0)
        lse = []
        delta = []
        for h in range(GROUP):
            prod = do_ref[rows, cols[h]].astype(F32) * o_ref[rows, cols[h]].astype(F32)
            delta.append(jnp.sum(prod.T, axis=0, keepdims=True))
            lse.append(lse_ref[h : h + 1, rows])
        dq = None
        for s in range(5):
            c = b + s
            half = slice(BLK * (c % 2), BLK * (c % 2) + BLK)
            k = tables[c][half, :HD]
            v = tables[c][half, HD:]
            scores = dot(k, q, NT)
            prob_grad = dot(v, do, NT)
            p_parts = []
            g_parts = []
            for h in range(GROUP):
                at = slice(BLK * h, BLK * h + BLK)
                p = jnp.exp(scores[:, at] * scaling - lse[h])
                if s == 4:
                    p = jnp.where(causal, p, 0.0)
                else:
                    m = 3 - s
                    used = picks_ref[0, b, h] == m
                    for t in range(1, 3):
                        used = used | (picks_ref[t, b, h] == m)
                    used = used & (first + b - 1 - m >= 0)
                    p = jnp.where(used, p, 0.0)
                p_parts.append(p.astype(BF))
                g_parts.append((p * (prob_grad[:, at] - delta[h])).astype(BF))
            p_half = jnp.concatenate(p_parts, axis=1)
            g_half = jnp.concatenate(g_parts, axis=1)
            part = dot(g_half, k, TN)
            dq = part if dq is None else dq + part
            k_part = dot(g_half, q, NN)
            v_part = dot(p_half, do, NN)
            dk[c] = k_part if dk[c] is None else dk[c] + k_part
            dv[c] = v_part if dv[c] is None else dv[c] + v_part
        for h in range(GROUP):
            aq_ref[rows, cols[h]] = (dq[BLK * h : BLK * h + BLK] * scaling).astype(BF)
    for c in range(6):
        half = slice(BLK * (c % 2), BLK * (c % 2) + BLK)
        sums[c][half, :HD] = (dk[c] * scaling).astype(sums[c].dtype)
        sums[c][half, HD:] = dv[c].astype(sums[c].dtype)


def attention(picks, q, do, o, lse, kv0, kv1, kv2):
    tokens = q.shape[0]
    vm = pl.BlockSpec(memory_space=pltpu.VMEM)
    sm = pl.BlockSpec(memory_space=pltpu.SMEM)
    return pl.pallas_call(
        attention_kernel,
        out_shape=(
            jax.ShapeDtypeStruct(q.shape, BF),
            jax.ShapeDtypeStruct((tokens, 2 * HD), F32),
            jax.ShapeDtypeStruct((tokens, 2 * HD), BF),
            jax.ShapeDtypeStruct((tokens, 2 * HD), BF),
        ),
        in_specs=[sm] + [vm] * 7,
        out_specs=(vm,) * 4,
        name="attention",
    )(
        picks.transpose(2, 0, 1), q, do, o, lse, kv0,
        placed_in(kv1, pltpu.VMEM), placed_in(kv2, pltpu.VMEM),
    )


def project_kernel(a_hbm, own_hbm, other_ref, out_hbm, a_ref, w_ref, out_ref, a_sem, w_sem, out_sem):
    zl = lax.axis_index("zl")
    load_a = pltpu.make_async_copy(a_hbm, a_ref, a_sem)
    load_a.start()
    loads = []
    for head in range(8):
        for e in range(2):
            k = lax.rem(2 * (head % 2) + e + 4 - zl, 4)
            loads.append(
                pltpu.make_async_copy(
                    own_hbm.at[k, head // 2], w_ref.at[head, e], w_sem.at[head, e]
                )
            )
            loads[-1].start()
    load_a.wait()
    stores = []
    for head in range(8):
        wide = []
        for e in range(2):
            loads[2 * head + e].wait()
            k = lax.rem(2 * (head % 2) + e + 4 - zl, 4)
            wide += [w_ref[head, e], other_ref[k, head // 2]]
        part = dot(a_ref[...], jnp.concatenate(wide, axis=0), NT).astype(BF)
        for r in range(2):
            at = 8 * r + head
            out_ref[at] = part[256 * r : 256 * r + 256]
            stores.append(pltpu.make_async_copy(out_ref.at[at], out_hbm.at[at], out_sem.at[at]))
            stores[-1].start()
    for store in stores:
        store.wait()


def placed_in(x, space):
    return pltpu.with_memory_space_constraint(x, space)


def project(a, wc, wo):
    hbm = pl.BlockSpec(memory_space=pltpu.HBM)
    rows, cols = wc.shape[2:]
    a = a.reshape(-1, a.shape[2])
    return pl.pallas_call(
        project_kernel,
        out_shape=jax.ShapeDtypeStruct((16, 256, 4 * rows), BF),
        in_specs=[hbm, hbm, pl.BlockSpec(memory_space=pltpu.VMEM)],
        out_specs=hbm,
        scratch_shapes=[
            pltpu.VMEM(a.shape, BF),
            pltpu.VMEM((8, 2, rows, cols), BF),
            pltpu.VMEM((16, 256, 4 * rows), BF),
            pltpu.SemaphoreType.DMA,
            pltpu.SemaphoreType.DMA((8, 2)),
            pltpu.SemaphoreType.DMA((16,)),
        ],
        name="project",
    )(a, wc, placed_in(wo, pltpu.VMEM))


def total_kernel(in_ref, out_ref):
    swapped = lax.axis_index("core") == 1
    for xh in range(2):
        total = in_ref[8 * xh].astype(F32)
        for h in range(1, 8):
            total = total + in_ref[8 * xh + h].astype(F32)
        for e in range(2):
            at = 256 * e + 128 * xh
            tile = total[:, 128 * e : 128 * e + 128]
            tile = jnp.where(swapped, pltpu.roll(tile, 64, 1), tile)
            out_ref[:, at : at + 128] = tile.astype(BF)


def totalled(parts):
    vm = pl.BlockSpec(memory_space=pltpu.VMEM)
    return pl.pallas_call(
        total_kernel,
        out_shape=jax.ShapeDtypeStruct((parts.shape[1], 512), BF),
        in_specs=[vm],
        out_specs=vm,
        name="total",
    )(placed_in(parts, pltpu.VMEM))


def prepare_kernel(k_ref, v_ref, qw_ref, kw_ref, vw_ref, kv_ref, w_ref):
    kv_ref[:, :HD] = k_ref[...]
    kv_ref[:, HD:] = v_ref[...]
    w_ref[:, : GROUP * HD] = qw_ref[...]
    w_ref[:, GROUP * HD : GROUP * HD + HD] = kw_ref[...]
    w_ref[:, GROUP * HD + HD :] = vw_ref[...]


def prepared(keys, values, qw, kw, vw):
    vm = pl.BlockSpec(memory_space=pltpu.VMEM)
    return pl.pallas_call(
        prepare_kernel,
        out_shape=(
            jax.ShapeDtypeStruct((keys.shape[0], 2 * HD), BF),
            jax.ShapeDtypeStruct((qw.shape[0], qw.shape[1] + 2 * HD), BF),
        ),
        in_specs=[vm] * 5,
        out_specs=(vm, vm),
        name="prepare",
    )(keys, values, qw, kw, vw)


def per_device(
    queries, key_rows, value_rows, attn_out, out_grad, log_sums, block_picks,
    query_weight, key_weight, value_weight,
):
    kv0, weight = prepared(key_rows, value_rows, query_weight, key_weight, value_weight)
    kv1 = passed_along(kv0, CTX, 1)
    kv2 = passed_along(kv0, CTX, 2)
    w0 = lax.all_gather(weight, "zh")
    w1 = shifted(w0, Z, -1)
    w3 = shifted(w0, Z, 1)
    w2 = lax.ppermute(w0, Z, [((z + 2 if z % 2 == 0 else z - 2) % 16, z) for z in range(16)])
    aq, own, ret1, ret2 = attention(
        block_picks, queries, out_grad, attn_out, log_sums, kv0, kv1, kv2
    )
    back1 = passed_along(ret1, CTX, -1)
    back2 = passed_along(ret2, CTX, -2)
    wc = jnp.stack([w0, w1, w2, w3])
    wo = shifted(wc, "core", 1)
    akv = (own + back1.astype(F32) + back2.astype(F32)).astype(BF)
    a_all = lax.all_gather(jnp.concatenate([aq, akv], axis=1), "xh")
    parts = project(a_all, wc, wo)
    parts = lax.all_to_all(parts, ("xh", "xl", "y"), 0, 0)
    return totalled(parts)


def solution(mesh):
    wide = Mesh(
        mesh.devices.reshape(4, 4, 2, 2, 2, 4), ("zh", "zl", "xh", "core", "xl", "y")
    )
    both = P(CTX, HEAD)
    placed = (both,) * 5 + (P(HEAD, CTX), P(CTX, HEAD, None)) + (both,) * 3
    return jax.shard_map(
        per_device, mesh=wide, in_specs=placed, out_specs=both, check_vma=False
    )
```

```python
import functools
import math

import jax
import jax.numpy as jnp
from jax import lax
from jax.experimental import pallas as pl
from jax.experimental.pallas import tpu as pltpu
from jax.sharding import Mesh
from jax.sharding import PartitionSpec as P


BLK = 128
HD = 128
GROUP = 4
BF = jnp.bfloat16
F32 = jnp.float32
Z = ("zh", "zl")
CTX = ("zh", "zl", "xh", "core")
HEAD = ("xl", "y")
NT = (((1,), (1,)), ((), ()))
NN = (((1,), (0,)), ((), ()))
TN = (((0,), (0,)), ((), ()))


def dot(a, b, dims):
    return lax.dot_general(a, b, dims, preferred_element_type=F32)


def passed_along(x, axis, by):
    n = lax.axis_size(axis)
    pairs = [(i, i + by) for i in range(n) if 0 <= i + by < n]
    return lax.ppermute(x, axis, pairs)


def shifted(x, axis, by):
    n = lax.axis_size(axis)
    return lax.ppermute(x, axis, [(i, (i + by) % n) for i in range(n)])


def attention_kernel(
    picks_ref, q_ref, do_ref, o_ref, lse_ref, kv0_ref, kv1_ref, kv2_ref,
    aq_ref, own_ref, ret1_ref, ret2_ref,
):
    scaling = 1.0 / math.sqrt(HD)
    first = lax.axis_index(CTX) * 2
    tables = (kv2_ref, kv2_ref, kv1_ref, kv1_ref, kv0_ref, kv0_ref)
    sums = (ret2_ref, ret2_ref, ret1_ref, ret1_ref, own_ref, own_ref)
    key_at = lax.broadcasted_iota(jnp.int32, (BLK, BLK), 0)
    query_at = lax.broadcasted_iota(jnp.int32, (BLK, BLK), 1)
    causal = key_at <= query_at
    dk = [None] * 6
    dv = [None] * 6
    for b in range(2):
        rows = slice(BLK * b, BLK * b + BLK)
        cols = [slice(HD * h, HD * h + HD) for h in range(GROUP)]
        q = jnp.concatenate([q_ref[rows, c] for c in cols], axis=0)
        do = jnp.concatenate([do_ref[rows, c] for c in cols], axis=0)
        lse = []
        delta = []
        for h in range(GROUP):
            prod = do_ref[rows, cols[h]].astype(F32) * o_ref[rows, cols[h]].astype(F32)
            delta.append(jnp.sum(prod.T, axis=0, keepdims=True))
            lse.append(lse_ref[h : h + 1, rows])
        dq = None
        for s in range(5):
            c = b + s
            half = slice(BLK * (c % 2), BLK * (c % 2) + BLK)
            k = tables[c][half, :HD]
            v = tables[c][half, HD:]
            scores = dot(k, q, NT)
            prob_grad = dot(v, do, NT)
            p_parts = []
            g_parts = []
            for h in range(GROUP):
                at = slice(BLK * h, BLK * h + BLK)
                p = jnp.exp(scores[:, at] * scaling - lse[h])
                if s == 4:
                    p = jnp.where(causal, p, 0.0)
                else:
                    m = 3 - s
                    used = picks_ref[0, b, h] == m
                    for t in range(1, 3):
                        used = used | (picks_ref[t, b, h] == m)
                    used = used & (first + b - 1 - m >= 0)
                    p = jnp.where(used, p, 0.0)
                p_parts.append(p.astype(BF))
                g_parts.append((p * (prob_grad[:, at] - delta[h])).astype(BF))
            p_half = jnp.concatenate(p_parts, axis=1)
            g_half = jnp.concatenate(g_parts, axis=1)
            part = dot(g_half, k, TN)
            dq = part if dq is None else dq + part
            k_part = dot(g_half, q, NN)
            v_part = dot(p_half, do, NN)
            dk[c] = k_part if dk[c] is None else dk[c] + k_part
            dv[c] = v_part if dv[c] is None else dv[c] + v_part
        for h in range(GROUP):
            aq_ref[rows, cols[h]] = (dq[BLK * h : BLK * h + BLK] * scaling).astype(BF)
    for c in range(6):
        half = slice(BLK * (c % 2), BLK * (c % 2) + BLK)
        sums[c][half, :HD] = (dk[c] * scaling).astype(sums[c].dtype)
        sums[c][half, HD:] = dv[c].astype(sums[c].dtype)


def attention(picks, q, do, o, lse, kv0, kv1, kv2):
    tokens = q.shape[0]
    vm = pl.BlockSpec(memory_space=pltpu.VMEM)
    sm = pl.BlockSpec(memory_space=pltpu.SMEM)
    return pl.pallas_call(
        attention_kernel,
        out_shape=(
            pltpu.VMEM(q.shape, BF),
            pltpu.VMEM((tokens, 2 * HD), F32),
            pltpu.VMEM((tokens, 2 * HD), BF),
            pltpu.VMEM((tokens, 2 * HD), BF),
        ),
        in_specs=[sm] + [vm] * 7,
        out_specs=(vm,) * 4,
        name="attention",
    )(
        picks.transpose(2, 0, 1), q, do, o, lse, placed_in(kv0, pltpu.VMEM),
        placed_in(kv1, pltpu.VMEM), placed_in(kv2, pltpu.VMEM),
    )


def project_kernel(side, q_ref, kv_ref, own_hbm, other_ref, *rest):
    out_hbm, w_ref, out_ref, w_sem, out_sem = rest[-5:]
    zl = lax.axis_index("zl")
    xh = lax.axis_index("xh")
    rows_of = xh if side == 0 else 1 - xh
    loads = [
        pltpu.make_async_copy(own_hbm.at[:, zh], w_ref.at[:, zh], w_sem.at[zh]) for zh in range(4)
    ]
    for load in loads:
        load.start()
    stores = []
    for head in range(8):
        zh = head // 2
        if head % 2 == 0:
            loads[zh].wait()
        wide = []
        for e in range(2):
            k = lax.rem(2 * (head % 2) + e + 4 - zl, 4)
            wide += [w_ref[k, zh], other_ref[k, zh]]
        w = jnp.concatenate(wide, axis=0)
        part = dot(q_ref[...], w[:, : GROUP * HD], NT) + dot(kv_ref[...], w[:, GROUP * HD :], NT)
        out_ref[head] = part.astype(BF)
        target = 4 * (head % 4) + 2 * (head // 4) + rows_of
        stores.append(
            pltpu.make_async_copy(out_ref.at[head], out_hbm.at[target], out_sem.at[head])
        )
        stores[-1].start()
    for store in stores:
        store.wait()


def placed_in(x, space):
    return pltpu.with_memory_space_constraint(x, space)


def project(side, aq, akv, wc, wo, parts=None):
    hbm = pl.BlockSpec(memory_space=pltpu.HBM)
    vm = pl.BlockSpec(memory_space=pltpu.VMEM)
    rows, _ = wc.shape[2:]
    extra = () if parts is None else (parts,)
    return pl.pallas_call(
        functools.partial(project_kernel, side),
        out_shape=jax.ShapeDtypeStruct((16, 256, 4 * rows), BF),
        in_specs=[vm, vm, hbm, vm] + [hbm] * len(extra),
        out_specs=hbm,
        scratch_shapes=[
            pltpu.VMEM(wc.shape, BF),
            pltpu.VMEM((8, 256, 4 * rows), BF),
            pltpu.SemaphoreType.DMA((4,)),
            pltpu.SemaphoreType.DMA((8,)),
        ],
        input_output_aliases={4: 0} if extra else {},
    )(placed_in(aq, pltpu.VMEM), placed_in(akv, pltpu.VMEM), wc, placed_in(wo, pltpu.VMEM), *extra)


def total_kernel(in_ref, out_ref):
    swapped = lax.axis_index("core") == 1
    for xh in range(2):
        total = in_ref[xh].astype(F32)
        for h in range(1, 8):
            total = total + in_ref[2 * h + xh].astype(F32)
        for e in range(2):
            at = 256 * e + 128 * xh
            tile = total[:, 128 * e : 128 * e + 128]
            tile = jnp.where(swapped, pltpu.roll(tile, 64, 1), tile)
            out_ref[:, at : at + 128] = tile.astype(BF)


def totalled(parts):
    vm = pl.BlockSpec(memory_space=pltpu.VMEM)
    return pl.pallas_call(
        total_kernel,
        out_shape=jax.ShapeDtypeStruct((parts.shape[1], 512), BF),
        in_specs=[vm],
        out_specs=vm,
        name="total",
    )(placed_in(parts, pltpu.VMEM))


def prepare_kernel(k_ref, v_ref, qw_ref, kw_ref, vw_ref, kv_ref, w_ref):
    kv_ref[:, :HD] = k_ref[...]
    kv_ref[:, HD:] = v_ref[...]
    w_ref[:, : GROUP * HD] = qw_ref[...]
    w_ref[:, GROUP * HD : GROUP * HD + HD] = kw_ref[...]
    w_ref[:, GROUP * HD + HD :] = vw_ref[...]


def prepared(keys, values, qw, kw, vw):
    vm = pl.BlockSpec(memory_space=pltpu.VMEM)
    return pl.pallas_call(
        prepare_kernel,
        out_shape=(
            pltpu.VMEM((keys.shape[0], 2 * HD), BF),
            pltpu.VMEM((qw.shape[0], qw.shape[1] + 2 * HD), BF),
        ),
        in_specs=[vm] * 5,
        out_specs=(vm, vm),
        name="prepare",
    )(keys, values, qw, kw, vw)


def per_device(
    queries, key_rows, value_rows, attn_out, out_grad, log_sums, block_picks,
    query_weight, key_weight, value_weight,
):
    kv0, weight = prepared(key_rows, value_rows, query_weight, key_weight, value_weight)
    w0 = lax.all_gather(weight, "zh")
    kv0, w0 = lax.optimization_barrier((kv0, w0))
    kv1 = passed_along(kv0, CTX, 1)
    kv2 = passed_along(kv0, CTX, 2)
    w1 = shifted(w0, Z, -1)
    w3 = shifted(w0, Z, 1)
    w2 = lax.ppermute(w0, Z, [((z + 2 if z % 2 == 0 else z - 2) % 16, z) for z in range(16)])
    aq, own, ret1, ret2 = attention(
        block_picks, queries, out_grad, attn_out, log_sums, kv0, kv1, kv2
    )
    back1 = passed_along(ret1, CTX, -1)
    back2 = passed_along(ret2, CTX, -2)
    aq_far = shifted(aq, "xh", 1)
    wc = jnp.stack([w0, w1, w2, w3])
    wo = shifted(wc, "core", 1)
    akv = (own + back1.astype(F32) + back2.astype(F32)).astype(BF)
    akv_far = shifted(akv, "xh", 1)
    parts = project(0, aq, akv, wc, wo)
    parts = project(1, aq_far, akv_far, wc, wo, parts)
    parts = lax.all_to_all(parts, ("y", "xl", "xh"), 0, 0)
    return totalled(parts)


def solution(mesh):
    wide = Mesh(
        mesh.devices.reshape(4, 4, 2, 2, 2, 4), ("zh", "zl", "xh", "core", "xl", "y")
    )
    both = P(CTX, HEAD)
    placed = (both,) * 5 + (P(HEAD, CTX), P(CTX, HEAD, None)) + (both,) * 3
    return jax.shard_map(per_device, mesh=wide, in_specs=placed, out_specs=both, check_vma=False)
```

```python
import functools
import math

import jax
import jax.numpy as jnp
from jax import lax
from jax.experimental import pallas as pl
from jax.experimental.pallas import tpu as pltpu
from jax.sharding import Mesh
from jax.sharding import PartitionSpec as P


BLK = 128
HD = 128
GROUP = 4
BF = jnp.bfloat16
F32 = jnp.float32
Z = ("zh", "zl")
CTX = ("zh", "zl", "xh", "core")
HEAD = ("xl", "y")
NT = (((1,), (1,)), ((), ()))
NN = (((1,), (0,)), ((), ()))
TN = (((0,), (0,)), ((), ()))


def dot(a, b, dims):
    return lax.dot_general(a, b, dims, preferred_element_type=F32)


def passed_along(x, axis, by):
    n = lax.axis_size(axis)
    pairs = [(i, i + by) for i in range(n) if 0 <= i + by < n]
    return lax.ppermute(x, axis, pairs)


def shifted(x, axis, by):
    n = lax.axis_size(axis)
    return lax.ppermute(x, axis, [(i, (i + by) % n) for i in range(n)])


def attention_kernel(
    picks_ref, q_ref, do_ref, o_ref, lse_ref, kv0_ref, kv1_ref, kv2_ref,
    aq_ref, own_ref, ret1_ref, ret2_ref,
):
    scaling = 1.0 / math.sqrt(HD)
    first = lax.axis_index(CTX) * 2
    tables = (kv2_ref, kv2_ref, kv1_ref, kv1_ref, kv0_ref, kv0_ref)
    sums = (ret2_ref, ret2_ref, ret1_ref, ret1_ref, own_ref, own_ref)
    key_at = lax.broadcasted_iota(jnp.int32, (BLK, BLK), 0)
    query_at = lax.broadcasted_iota(jnp.int32, (BLK, BLK), 1)
    causal = key_at <= query_at
    dk = [None] * 6
    dv = [None] * 6
    for b in range(2):
        rows = slice(BLK * b, BLK * b + BLK)
        cols = [slice(HD * h, HD * h + HD) for h in range(GROUP)]
        q = jnp.concatenate([q_ref[rows, c] for c in cols], axis=0)
        do = jnp.concatenate([do_ref[rows, c] for c in cols], axis=0)
        lse = []
        delta = []
        for h in range(GROUP):
            prod = do_ref[rows, cols[h]].astype(F32) * o_ref[rows, cols[h]].astype(F32)
            delta.append(jnp.sum(prod.T, axis=0, keepdims=True))
            lse.append(lse_ref[h : h + 1, rows])
        dq = None
        for s in range(5):
            c = b + s
            half = slice(BLK * (c % 2), BLK * (c % 2) + BLK)
            k = tables[c][half, :HD]
            v = tables[c][half, HD:]
            scores = dot(k, q, NT)
            prob_grad = dot(v, do, NT)
            p_parts = []
            g_parts = []
            for h in range(GROUP):
                at = slice(BLK * h, BLK * h + BLK)
                p = jnp.exp(scores[:, at] * scaling - lse[h])
                if s == 4:
                    p = jnp.where(causal, p, 0.0)
                else:
                    m = 3 - s
                    used = picks_ref[0, b, h] == m
                    for t in range(1, 3):
                        used = used | (picks_ref[t, b, h] == m)
                    used = used & (first + b - 1 - m >= 0)
                    p = jnp.where(used, p, 0.0)
                p_parts.append(p.astype(BF))
                g_parts.append((p * (prob_grad[:, at] - delta[h])).astype(BF))
            p_half = jnp.concatenate(p_parts, axis=1)
            g_half = jnp.concatenate(g_parts, axis=1)
            part = dot(g_half, k, TN)
            dq = part if dq is None else dq + part
            k_part = dot(g_half, q, NN)
            v_part = dot(p_half, do, NN)
            dk[c] = k_part if dk[c] is None else dk[c] + k_part
            dv[c] = v_part if dv[c] is None else dv[c] + v_part
        for h in range(GROUP):
            aq_ref[rows, cols[h]] = (dq[BLK * h : BLK * h + BLK] * scaling).astype(BF)
    for c in range(6):
        half = slice(BLK * (c % 2), BLK * (c % 2) + BLK)
        sums[c][half, :HD] = (dk[c] * scaling).astype(sums[c].dtype)
        sums[c][half, HD:] = dv[c].astype(sums[c].dtype)


def attention(picks, q, do, o, lse, kv0, kv1, kv2):
    tokens = q.shape[0]
    vm = pl.BlockSpec(memory_space=pltpu.VMEM)
    sm = pl.BlockSpec(memory_space=pltpu.SMEM)
    return pl.pallas_call(
        attention_kernel,
        out_shape=(
            pltpu.VMEM(q.shape, BF),
            pltpu.VMEM((tokens, 2 * HD), F32),
            pltpu.VMEM((tokens, 2 * HD), BF),
            pltpu.VMEM((tokens, 2 * HD), BF),
        ),
        in_specs=[sm] + [vm] * 7,
        out_specs=(vm,) * 4,
        name="attention",
    )(
        picks.transpose(2, 0, 1), q, do, o, lse, placed_in(kv0, pltpu.VMEM),
        placed_in(kv1, pltpu.VMEM), placed_in(kv2, pltpu.VMEM),
    )


def project_kernel(side, q_ref, kv_ref, own_hbm, other_ref, *rest):
    out_hbm, w_ref, out_ref, w_sem, out_sem = rest[-5:]
    zl = lax.axis_index("zl")
    xh = lax.axis_index("xh")
    first = 8 * (xh if side == 0 else 1 - xh)
    loads = [
        pltpu.make_async_copy(own_hbm.at[:, zh], w_ref.at[:, zh], w_sem.at[zh]) for zh in range(4)
    ]
    for load in loads:
        load.start()
    stores = []
    for head in range(8):
        zh = head // 2
        if head % 2 == 0:
            loads[zh].wait()
        wide = []
        for e in range(2):
            k = lax.rem(2 * (head % 2) + e + 4 - zl, 4)
            wide += [w_ref[k, zh], other_ref[k, zh]]
        w = jnp.concatenate(wide, axis=0)
        part = dot(q_ref[...], w[:, : GROUP * HD], NT) + dot(kv_ref[...], w[:, GROUP * HD :], NT)
        out_ref[head] = part.astype(BF)
        stores.append(
            pltpu.make_async_copy(out_ref.at[head], out_hbm.at[first + head], out_sem.at[head])
        )
        stores[-1].start()
    for store in stores:
        store.wait()


def placed_in(x, space):
    return pltpu.with_memory_space_constraint(x, space)


def project(side, aq, akv, wc, wo, parts=None):
    hbm = pl.BlockSpec(memory_space=pltpu.HBM)
    vm = pl.BlockSpec(memory_space=pltpu.VMEM)
    rows, _ = wc.shape[2:]
    extra = () if parts is None else (parts,)
    return pl.pallas_call(
        functools.partial(project_kernel, side),
        out_shape=jax.ShapeDtypeStruct((16, 256, 4 * rows), BF),
        in_specs=[vm, vm, hbm, vm] + [hbm] * len(extra),
        out_specs=hbm,
        scratch_shapes=[
            pltpu.VMEM(wc.shape, BF),
            pltpu.VMEM((8, 256, 4 * rows), BF),
            pltpu.SemaphoreType.DMA((4,)),
            pltpu.SemaphoreType.DMA((8,)),
        ],
        input_output_aliases={4: 0} if extra else {},
    )(placed_in(aq, pltpu.VMEM), placed_in(akv, pltpu.VMEM), wc, placed_in(wo, pltpu.VMEM), *extra)


def total_kernel(in_ref, out_ref):
    swapped = lax.axis_index("core") == 1
    for xh in range(2):
        total = in_ref[8 * xh].astype(F32)
        for h in range(1, 8):
            total = total + in_ref[8 * xh + h].astype(F32)
        for e in range(2):
            at = 256 * e + 128 * xh
            tile = total[:, 128 * e : 128 * e + 128]
            tile = jnp.where(swapped, pltpu.roll(tile, 64, 1), tile)
            out_ref[:, at : at + 128] = tile.astype(BF)


def totalled(parts):
    vm = pl.BlockSpec(memory_space=pltpu.VMEM)
    return pl.pallas_call(
        total_kernel,
        out_shape=jax.ShapeDtypeStruct((parts.shape[1], 512), BF),
        in_specs=[vm],
        out_specs=vm,
        name="total",
    )(placed_in(parts, pltpu.VMEM))


def prepare_kernel(k_ref, v_ref, qw_ref, kw_ref, vw_ref, kv_ref, w_ref):
    kv_ref[:, :HD] = k_ref[...]
    kv_ref[:, HD:] = v_ref[...]
    w_ref[:, : GROUP * HD] = qw_ref[...]
    w_ref[:, GROUP * HD : GROUP * HD + HD] = kw_ref[...]
    w_ref[:, GROUP * HD + HD :] = vw_ref[...]


def prepared(keys, values, qw, kw, vw):
    vm = pl.BlockSpec(memory_space=pltpu.VMEM)
    return pl.pallas_call(
        prepare_kernel,
        out_shape=(
            pltpu.VMEM((keys.shape[0], 2 * HD), BF),
            pltpu.VMEM((qw.shape[0], qw.shape[1] + 2 * HD), BF),
        ),
        in_specs=[vm] * 5,
        out_specs=(vm, vm),
        name="prepare",
    )(keys, values, qw, kw, vw)


def per_device(
    queries, key_rows, value_rows, attn_out, out_grad, log_sums, block_picks,
    query_weight, key_weight, value_weight,
):
    kv0, weight = prepared(key_rows, value_rows, query_weight, key_weight, value_weight)
    kv1 = passed_along(kv0, CTX, 1)
    kv2 = passed_along(kv0, CTX, 2)
    w0 = lax.all_gather(weight, "zh")
    w1 = shifted(w0, Z, -1)
    w3 = shifted(w0, Z, 1)
    w2 = lax.ppermute(w0, Z, [((z + 2 if z % 2 == 0 else z - 2) % 16, z) for z in range(16)])
    aq, own, ret1, ret2 = attention(
        block_picks, queries, out_grad, attn_out, log_sums, kv0, kv1, kv2
    )
    back1 = passed_along(ret1, CTX, -1)
    back2 = passed_along(ret2, CTX, -2)
    aq_far = shifted(aq, "xh", 1)
    wc = jnp.stack([w0, w1, w2, w3])
    wo = shifted(wc, "core", 1)
    akv = (own + back1.astype(F32) + back2.astype(F32)).astype(BF)
    akv_far = shifted(akv, "xh", 1)
    parts = project(0, aq, akv, wc, wo)
    parts = project(1, aq_far, akv_far, wc, wo, parts)
    parts = lax.all_to_all(parts.transpose(1, 0, 2), ("xh", "xl", "y"), 1, 1)
    return totalled(parts.transpose(1, 0, 2))


def solution(mesh):
    wide = Mesh(
        mesh.devices.reshape(4, 4, 2, 2, 2, 4), ("zh", "zl", "xh", "core", "xl", "y")
    )
    both = P(CTX, HEAD)
    placed = (both,) * 5 + (P(HEAD, CTX), P(CTX, HEAD, None)) + (both,) * 3
    return jax.shard_map(per_device, mesh=wide, in_specs=placed, out_specs=both, check_vma=False)
```

```python
import functools
import math

import jax
import jax.numpy as jnp
from jax import lax
from jax.experimental import pallas as pl
from jax.experimental.pallas import tpu as pltpu
from jax.sharding import Mesh
from jax.sharding import PartitionSpec as P


BLK = 128
HD = 128
GROUP = 4
BF = jnp.bfloat16
F32 = jnp.float32
Z = ("zh", "zl")
CTX = ("zh", "zl", "xh", "core")
HEAD = ("xl", "y")
NT = (((1,), (1,)), ((), ()))
NN = (((1,), (0,)), ((), ()))
TN = (((0,), (0,)), ((), ()))


def dot(a, b, dims):
    return lax.dot_general(a, b, dims, preferred_element_type=F32)


def passed_along(x, axis, by):
    n = lax.axis_size(axis)
    pairs = [(i, i + by) for i in range(n) if 0 <= i + by < n]
    return lax.ppermute(x, axis, pairs)


def shifted(x, axis, by):
    n = lax.axis_size(axis)
    return lax.ppermute(x, axis, [(i, (i + by) % n) for i in range(n)])


def attention_kernel(
    picks_ref, q_ref, do_ref, o_ref, lse_ref, here_ref, prev_ref,
    aq_ref, own_ref, ret1_ref, ret2_ref,
):
    scaling = 1.0 / math.sqrt(HD)
    first = lax.axis_index(CTX) * 2
    core = lax.axis_index("core")

    def table(c, cols):
        half = slice(BLK * (c % 2), BLK * (c % 2) + BLK)
        if c < 2:
            return prev_ref[core, half, cols]
        if c < 4:
            return jnp.where(core == 0, prev_ref[1, half, cols], here_ref[0, half, cols])
        return here_ref[core, half, cols]

    sums = (ret2_ref, ret2_ref, ret1_ref, ret1_ref, own_ref, own_ref)
    key_at = lax.broadcasted_iota(jnp.int32, (BLK, BLK), 0)
    query_at = lax.broadcasted_iota(jnp.int32, (BLK, BLK), 1)
    causal = key_at <= query_at
    dk = [None] * 6
    dv = [None] * 6
    for b in range(2):
        rows = slice(BLK * b, BLK * b + BLK)
        cols = [slice(HD * h, HD * h + HD) for h in range(GROUP)]
        q = jnp.concatenate([q_ref[rows, c] for c in cols], axis=0)
        do = jnp.concatenate([do_ref[rows, c] for c in cols], axis=0)
        lse = []
        delta = []
        for h in range(GROUP):
            prod = do_ref[rows, cols[h]].astype(F32) * o_ref[rows, cols[h]].astype(F32)
            delta.append(jnp.sum(prod.T, axis=0, keepdims=True))
            lse.append(lse_ref[h : h + 1, rows])
        dq = None
        for s in range(5):
            c = b + s
            k = table(c, slice(0, HD))
            v = table(c, slice(HD, 2 * HD))
            scores = dot(k, q, NT)
            prob_grad = dot(v, do, NT)
            p_parts = []
            g_parts = []
            for h in range(GROUP):
                at = slice(BLK * h, BLK * h + BLK)
                p = jnp.exp(scores[:, at] * scaling - lse[h])
                if s == 4:
                    p = jnp.where(causal, p, 0.0)
                else:
                    m = 3 - s
                    used = picks_ref[0, b, h] == m
                    for t in range(1, 3):
                        used = used | (picks_ref[t, b, h] == m)
                    used = used & (first + b - 1 - m >= 0)
                    p = jnp.where(used, p, 0.0)
                p_parts.append(p.astype(BF))
                g_parts.append((p * (prob_grad[:, at] - delta[h])).astype(BF))
            p_half = jnp.concatenate(p_parts, axis=1)
            g_half = jnp.concatenate(g_parts, axis=1)
            part = dot(g_half, k, TN)
            dq = part if dq is None else dq + part
            k_part = dot(g_half, q, NN)
            v_part = dot(p_half, do, NN)
            dk[c] = k_part if dk[c] is None else dk[c] + k_part
            dv[c] = v_part if dv[c] is None else dv[c] + v_part
        for h in range(GROUP):
            aq_ref[rows, cols[h]] = (dq[BLK * h : BLK * h + BLK] * scaling).astype(BF)
    for c in range(6):
        half = slice(BLK * (c % 2), BLK * (c % 2) + BLK)
        sums[c][half, :HD] = (dk[c] * scaling).astype(sums[c].dtype)
        sums[c][half, HD:] = dv[c].astype(sums[c].dtype)


def attention(picks, q, do, o, lse, here, prev):
    tokens = q.shape[0]
    vm = pl.BlockSpec(memory_space=pltpu.VMEM)
    sm = pl.BlockSpec(memory_space=pltpu.SMEM)
    return pl.pallas_call(
        attention_kernel,
        out_shape=(
            pltpu.VMEM(q.shape, BF),
            pltpu.VMEM((tokens, 2 * HD), F32),
            pltpu.VMEM((tokens, 2 * HD), BF),
            pltpu.VMEM((tokens, 2 * HD), BF),
        ),
        in_specs=[sm] + [vm] * 6,
        out_specs=(vm,) * 4,
        name="attention",
    )(
        picks.transpose(2, 0, 1), q, do, o, lse,
        placed_in(here, pltpu.VMEM), placed_in(prev, pltpu.VMEM),
    )


def project_kernel(side, q_ref, kv_ref, own_hbm, other_ref, *rest):
    out_hbm, w_ref, out_ref, w_sem, out_sem = rest[-5:]
    zl = lax.axis_index("zl")
    xh = lax.axis_index("xh")
    first = 8 * (xh if side == 0 else 1 - xh)
    loads = [
        pltpu.make_async_copy(own_hbm.at[:, zh], w_ref.at[:, zh], w_sem.at[zh]) for zh in range(4)
    ]
    for load in loads:
        load.start()
    stores = []
    for head in range(8):
        zh = head // 2
        if head % 2 == 0:
            loads[zh].wait()
        wide = []
        for e in range(2):
            k = lax.rem(2 * (head % 2) + e + 4 - zl, 4)
            wide += [w_ref[k, zh], other_ref[k, zh]]
        w = jnp.concatenate(wide, axis=0)
        part = dot(q_ref[...], w[:, : GROUP * HD], NT) + dot(kv_ref[...], w[:, GROUP * HD :], NT)
        out_ref[head] = part.astype(BF)
        stores.append(
            pltpu.make_async_copy(out_ref.at[head], out_hbm.at[first + head], out_sem.at[head])
        )
        stores[-1].start()
    for store in stores:
        store.wait()


def placed_in(x, space):
    return pltpu.with_memory_space_constraint(x, space)


def project(side, aq, akv, wc, wo, parts=None):
    hbm = pl.BlockSpec(memory_space=pltpu.HBM)
    vm = pl.BlockSpec(memory_space=pltpu.VMEM)
    rows, _ = wc.shape[2:]
    extra = () if parts is None else (parts,)
    return pl.pallas_call(
        functools.partial(project_kernel, side),
        out_shape=jax.ShapeDtypeStruct((16, 256, 4 * rows), BF),
        in_specs=[vm, vm, hbm, vm] + [hbm] * len(extra),
        out_specs=hbm,
        scratch_shapes=[
            pltpu.VMEM(wc.shape, BF),
            pltpu.VMEM((8, 256, 4 * rows), BF),
            pltpu.SemaphoreType.DMA((4,)),
            pltpu.SemaphoreType.DMA((8,)),
        ],
        input_output_aliases={4: 0} if extra else {},
    )(placed_in(aq, pltpu.VMEM), placed_in(akv, pltpu.VMEM), wc, placed_in(wo, pltpu.VMEM), *extra)


def total_kernel(in_ref, out_ref):
    swapped = lax.axis_index("core") == 1
    for xh in range(2):
        total = in_ref[8 * xh].astype(F32)
        for h in range(1, 8):
            total = total + in_ref[8 * xh + h].astype(F32)
        for e in range(2):
            at = 256 * e + 128 * xh
            tile = total[:, 128 * e : 128 * e + 128]
            tile = jnp.where(swapped, pltpu.roll(tile, 64, 1), tile)
            out_ref[:, at : at + 128] = tile.astype(BF)


def totalled(parts):
    vm = pl.BlockSpec(memory_space=pltpu.VMEM)
    return pl.pallas_call(
        total_kernel,
        out_shape=jax.ShapeDtypeStruct((parts.shape[1], 512), BF),
        in_specs=[vm],
        out_specs=vm,
        name="total",
    )(placed_in(parts, pltpu.VMEM))


def prepare_kernel(k_ref, v_ref, qw_ref, kw_ref, vw_ref, kv_ref, w_ref):
    kv_ref[:, :HD] = k_ref[...]
    kv_ref[:, HD:] = v_ref[...]
    w_ref[:, : GROUP * HD] = qw_ref[...]
    w_ref[:, GROUP * HD : GROUP * HD + HD] = kw_ref[...]
    w_ref[:, GROUP * HD + HD :] = vw_ref[...]


def prepared(keys, values, qw, kw, vw):
    vm = pl.BlockSpec(memory_space=pltpu.VMEM)
    return pl.pallas_call(
        prepare_kernel,
        out_shape=(
            pltpu.VMEM((keys.shape[0], 2 * HD), BF),
            pltpu.VMEM((qw.shape[0], qw.shape[1] + 2 * HD), BF),
        ),
        in_specs=[vm] * 5,
        out_specs=(vm, vm),
        name="prepare",
    )(keys, values, qw, kw, vw)


def per_device(
    queries, key_rows, value_rows, attn_out, out_grad, log_sums, block_picks,
    query_weight, key_weight, value_weight,
):
    kv0, weight = prepared(key_rows, value_rows, query_weight, key_weight, value_weight)
    here = lax.all_gather(kv0, "core")
    prev = passed_along(here, CTX, 2)
    w0 = lax.all_gather(weight, "zh")
    w1 = shifted(w0, Z, -1)
    w3 = shifted(w0, Z, 1)
    w2 = lax.ppermute(w0, Z, [((z + 2 if z % 2 == 0 else z - 2) % 16, z) for z in range(16)])
    aq, own, ret1, ret2 = attention(block_picks, queries, out_grad, attn_out, log_sums, here, prev)
    back1 = passed_along(ret1, CTX, -1)
    back2 = passed_along(ret2, CTX, -2)
    aq_far = shifted(aq, "xh", 1)
    wc = jnp.stack([w0, w1, w2, w3])
    wo = shifted(wc, "core", 1)
    akv = (own + back1.astype(F32) + back2.astype(F32)).astype(BF)
    akv_far = shifted(akv, "xh", 1)
    parts = project(0, aq, akv, wc, wo)
    parts = project(1, aq_far, akv_far, wc, wo, parts)
    parts = lax.all_to_all(parts, ("xh", "xl", "y"), 0, 0)
    return totalled(parts)


def solution(mesh):
    wide = Mesh(
        mesh.devices.reshape(4, 4, 2, 2, 2, 4), ("zh", "zl", "xh", "core", "xl", "y")
    )
    both = P(CTX, HEAD)
    placed = (both,) * 5 + (P(HEAD, CTX), P(CTX, HEAD, None)) + (both,) * 3
    return jax.shard_map(per_device, mesh=wide, in_specs=placed, out_specs=both, check_vma=False)
```

```python
import functools
import math

import jax
import jax.numpy as jnp
from jax import lax
from jax.experimental import pallas as pl
from jax.experimental.pallas import tpu as pltpu
from jax.sharding import Mesh
from jax.sharding import PartitionSpec as P


BLK = 128
HD = 128
GROUP = 4
BF = jnp.bfloat16
F32 = jnp.float32
Z = ("zh", "zl")
CTX = ("zh", "zl", "xh", "core")
HEAD = ("xl", "y")
NT = (((1,), (1,)), ((), ()))
NN = (((1,), (0,)), ((), ()))
TN = (((0,), (0,)), ((), ()))


def dot(a, b, dims):
    return lax.dot_general(a, b, dims, preferred_element_type=F32)


def passed_along(x, axis, by):
    n = lax.axis_size(axis)
    pairs = [(i, i + by) for i in range(n) if 0 <= i + by < n]
    return lax.ppermute(x, axis, pairs)


def shifted(x, axis, by):
    n = lax.axis_size(axis)
    return lax.ppermute(x, axis, [(i, (i + by) % n) for i in range(n)])


def attention_kernel(
    picks_ref, q_ref, do_ref, o_ref, lse_ref, kv0_ref, kv1_ref, kv2_ref,
    aq_ref, own_ref, ret1_ref, ret2_ref,
):
    scaling = 1.0 / math.sqrt(HD)
    first = lax.axis_index(CTX) * 2
    tables = (kv2_ref, kv2_ref, kv1_ref, kv1_ref, kv0_ref, kv0_ref)
    sums = (ret2_ref, ret2_ref, ret1_ref, ret1_ref, own_ref, own_ref)
    key_at = lax.broadcasted_iota(jnp.int32, (BLK, BLK), 0)
    query_at = lax.broadcasted_iota(jnp.int32, (BLK, BLK), 1)
    causal = key_at <= query_at
    dk = [None] * 6
    dv = [None] * 6
    for b in range(2):
        rows = slice(BLK * b, BLK * b + BLK)
        cols = [slice(HD * h, HD * h + HD) for h in range(GROUP)]
        q = jnp.concatenate([q_ref[rows, c] for c in cols], axis=0)
        do = jnp.concatenate([do_ref[rows, c] for c in cols], axis=0)
        lse = []
        delta = []
        for h in range(GROUP):
            prod = do_ref[rows, cols[h]].astype(F32) * o_ref[rows, cols[h]].astype(F32)
            delta.append(jnp.sum(prod.T, axis=0, keepdims=True))
            lse.append(lse_ref[h : h + 1, rows])
        keys = []
        g_all = []
        for s in range(5):
            c = b + s
            half = slice(BLK * (c % 2), BLK * (c % 2) + BLK)
            k = tables[c][half, :HD]
            v = tables[c][half, HD:]
            scores = dot(k, q, NT)
            prob_grad = dot(v, do, NT)
            p_parts = []
            g_parts = []
            for h in range(GROUP):
                at = slice(BLK * h, BLK * h + BLK)
                p = jnp.exp(scores[:, at] * scaling - lse[h])
                if s == 4:
                    p = jnp.where(causal, p, 0.0)
                else:
                    m = 3 - s
                    used = picks_ref[0, b, h] == m
                    for t in range(1, 3):
                        used = used | (picks_ref[t, b, h] == m)
                    used = used & (first + b - 1 - m >= 0)
                    p = jnp.where(used, p, 0.0)
                p_parts.append(p.astype(BF))
                g_parts.append((p * (prob_grad[:, at] - delta[h])).astype(BF))
            p_half = jnp.concatenate(p_parts, axis=1)
            g_half = jnp.concatenate(g_parts, axis=1)
            keys.append(k)
            g_all.append(g_half)
            k_part = dot(g_half, q, NN)
            v_part = dot(p_half, do, NN)
            dk[c] = k_part if dk[c] is None else dk[c] + k_part
            dv[c] = v_part if dv[c] is None else dv[c] + v_part
        dq = dot(jnp.concatenate(g_all, axis=0), jnp.concatenate(keys, axis=0), TN)
        for h in range(GROUP):
            aq_ref[rows, cols[h]] = (dq[BLK * h : BLK * h + BLK] * scaling).astype(BF)
    for c in range(6):
        half = slice(BLK * (c % 2), BLK * (c % 2) + BLK)
        sums[c][half, :HD] = (dk[c] * scaling).astype(sums[c].dtype)
        sums[c][half, HD:] = dv[c].astype(sums[c].dtype)


def attention(picks, q, do, o, lse, kv0, kv1, kv2):
    tokens = q.shape[0]
    vm = pl.BlockSpec(memory_space=pltpu.VMEM)
    sm = pl.BlockSpec(memory_space=pltpu.SMEM)
    return pl.pallas_call(
        attention_kernel,
        out_shape=(
            pltpu.VMEM(q.shape, BF),
            pltpu.VMEM((tokens, 2 * HD), F32),
            pltpu.VMEM((tokens, 2 * HD), BF),
            pltpu.VMEM((tokens, 2 * HD), BF),
        ),
        in_specs=[sm] + [vm] * 7,
        out_specs=(vm,) * 4,
        name="attention",
    )(
        picks.transpose(2, 0, 1), q, do, o, lse, placed_in(kv0, pltpu.VMEM),
        placed_in(kv1, pltpu.VMEM), placed_in(kv2, pltpu.VMEM),
    )


def project_kernel(side, q_ref, kv_ref, own_hbm, other_ref, *rest):
    out_hbm, w_ref, out_ref, w_sem, out_sem = rest[-5:]
    zl = lax.axis_index("zl")
    xh = lax.axis_index("xh")
    first = 8 * (xh if side == 0 else 1 - xh)
    loads = [
        pltpu.make_async_copy(own_hbm.at[:, zh], w_ref.at[:, zh], w_sem.at[zh]) for zh in range(4)
    ]
    for load in loads:
        load.start()
    a = jnp.concatenate([q_ref[...], kv_ref[...]], axis=1)
    stores = []
    for head in range(8):
        zh = head // 2
        if head % 2 == 0:
            loads[zh].wait()
        wide = []
        for e in range(2):
            k = lax.rem(2 * (head % 2) + e + 4 - zl, 4)
            wide += [w_ref[k, zh], other_ref[k, zh]]
        w = jnp.concatenate(wide, axis=0)
        out_ref[head] = dot(a, w, NT).astype(BF)
        stores.append(
            pltpu.make_async_copy(out_ref.at[head], out_hbm.at[first + head], out_sem.at[head])
        )
        stores[-1].start()
    for store in stores:
        store.wait()


def placed_in(x, space):
    return pltpu.with_memory_space_constraint(x, space)


def project(side, aq, akv, wc, wo, parts=None):
    hbm = pl.BlockSpec(memory_space=pltpu.HBM)
    vm = pl.BlockSpec(memory_space=pltpu.VMEM)
    rows, _ = wc.shape[2:]
    extra = () if parts is None else (parts,)
    return pl.pallas_call(
        functools.partial(project_kernel, side),
        out_shape=jax.ShapeDtypeStruct((16, 256, 4 * rows), BF),
        in_specs=[vm, vm, hbm, vm] + [hbm] * len(extra),
        out_specs=hbm,
        scratch_shapes=[
            pltpu.VMEM(wc.shape, BF),
            pltpu.VMEM((8, 256, 4 * rows), BF),
            pltpu.SemaphoreType.DMA((4,)),
            pltpu.SemaphoreType.DMA((8,)),
        ],
        input_output_aliases={4: 0} if extra else {},
    )(placed_in(aq, pltpu.VMEM), placed_in(akv, pltpu.VMEM), wc, placed_in(wo, pltpu.VMEM), *extra)


def total_kernel(in_ref, out_ref):
    swapped = lax.axis_index("core") == 1
    for xh in range(2):
        total = in_ref[8 * xh].astype(F32)
        for h in range(1, 8):
            total = total + in_ref[8 * xh + h].astype(F32)
        for e in range(2):
            at = 256 * e + 128 * xh
            tile = total[:, 128 * e : 128 * e + 128]
            tile = jnp.where(swapped, pltpu.roll(tile, 64, 1), tile)
            out_ref[:, at : at + 128] = tile.astype(BF)


def totalled(parts):
    vm = pl.BlockSpec(memory_space=pltpu.VMEM)
    return pl.pallas_call(
        total_kernel,
        out_shape=jax.ShapeDtypeStruct((parts.shape[1], 512), BF),
        in_specs=[vm],
        out_specs=vm,
        name="total",
    )(placed_in(parts, pltpu.VMEM))


def prepare_kernel(k_ref, v_ref, qw_ref, kw_ref, vw_ref, kv_ref, w_ref):
    kv_ref[:, :HD] = k_ref[...]
    kv_ref[:, HD:] = v_ref[...]
    w_ref[:, : GROUP * HD] = qw_ref[...]
    w_ref[:, GROUP * HD : GROUP * HD + HD] = kw_ref[...]
    w_ref[:, GROUP * HD + HD :] = vw_ref[...]


def prepared(keys, values, qw, kw, vw):
    vm = pl.BlockSpec(memory_space=pltpu.VMEM)
    return pl.pallas_call(
        prepare_kernel,
        out_shape=(
            pltpu.VMEM((keys.shape[0], 2 * HD), BF),
            pltpu.VMEM((qw.shape[0], qw.shape[1] + 2 * HD), BF),
        ),
        in_specs=[vm] * 5,
        out_specs=(vm, vm),
        name="prepare",
    )(keys, values, qw, kw, vw)


def per_device(
    queries, key_rows, value_rows, attn_out, out_grad, log_sums, block_picks,
    query_weight, key_weight, value_weight,
):
    kv0, weight = prepared(key_rows, value_rows, query_weight, key_weight, value_weight)
    kv1 = passed_along(kv0, CTX, 1)
    kv2 = passed_along(kv0, CTX, 2)
    w0 = lax.all_gather(weight, "zh")
    w1 = shifted(w0, Z, -1)
    w3 = shifted(w0, Z, 1)
    w2 = lax.ppermute(w0, Z, [((z + 2 if z % 2 == 0 else z - 2) % 16, z) for z in range(16)])
    aq, own, ret1, ret2 = attention(
        block_picks, queries, out_grad, attn_out, log_sums, kv0, kv1, kv2
    )
    back1 = passed_along(ret1, CTX, -1)
    back2 = passed_along(ret2, CTX, -2)
    aq_far = shifted(aq, "xh", 1)
    wc = jnp.stack([w0, w1, w2, w3])
    wo = shifted(wc, "core", 1)
    akv = (own + back1.astype(F32) + back2.astype(F32)).astype(BF)
    akv_far = shifted(akv, "xh", 1)
    parts = project(0, aq, akv, wc, wo)
    parts = project(1, aq_far, akv_far, wc, wo, parts)
    parts = lax.all_to_all(parts, ("xh", "xl", "y"), 0, 0)
    return totalled(parts)


def solution(mesh):
    wide = Mesh(
        mesh.devices.reshape(4, 4, 2, 2, 2, 4), ("zh", "zl", "xh", "core", "xl", "y")
    )
    both = P(CTX, HEAD)
    placed = (both,) * 5 + (P(HEAD, CTX), P(CTX, HEAD, None)) + (both,) * 3
    return jax.shard_map(
        per_device, mesh=wide, in_specs=placed, out_specs=both, check_vma=False
    )
```

```python
import functools
import math

import jax
import jax.numpy as jnp
from jax import lax
from jax.experimental import pallas as pl
from jax.experimental.pallas import tpu as pltpu
from jax.sharding import Mesh
from jax.sharding import PartitionSpec as P


BLK = 128
HD = 128
GROUP = 4
BF = jnp.bfloat16
F32 = jnp.float32
Z = ("zh", "zl")
CTX = ("zh", "zl", "xh", "core")
HEAD = ("xl", "y")
NT = (((1,), (1,)), ((), ()))
NN = (((1,), (0,)), ((), ()))
TN = (((0,), (0,)), ((), ()))


def dot(a, b, dims):
    return lax.dot_general(a, b, dims, preferred_element_type=F32)


def passed_along(x, axis, by):
    n = lax.axis_size(axis)
    pairs = [(i, i + by) for i in range(n) if 0 <= i + by < n]
    return lax.ppermute(x, axis, pairs)


def shifted(x, axis, by):
    n = lax.axis_size(axis)
    return lax.ppermute(x, axis, [(i, (i + by) % n) for i in range(n)])


def attention_kernel(
    picks_ref, q_ref, do_ref, o_ref, lse_ref, kv0_ref, kv1_ref, kv2_ref,
    aq_ref, own_ref, ret1_ref, ret2_ref,
):
    scaling = 1.0 / math.sqrt(HD)
    first = lax.axis_index(CTX) * 2
    tables = (kv2_ref, kv2_ref, kv1_ref, kv1_ref, kv0_ref, kv0_ref)
    sums = (ret2_ref, ret2_ref, ret1_ref, ret1_ref, own_ref, own_ref)
    key_at = lax.broadcasted_iota(jnp.int32, (BLK, BLK), 0)
    query_at = lax.broadcasted_iota(jnp.int32, (BLK, BLK), 1)
    causal = key_at <= query_at
    dk = [None] * 6
    dv = [None] * 6
    for b in range(2):
        rows = slice(BLK * b, BLK * b + BLK)
        cols = [slice(HD * h, HD * h + HD) for h in range(GROUP)]
        q = jnp.concatenate([q_ref[rows, c] for c in cols], axis=0)
        do = jnp.concatenate([do_ref[rows, c] for c in cols], axis=0)
        lse = []
        delta = []
        for h in range(GROUP):
            prod = do_ref[rows, cols[h]].astype(F32) * o_ref[rows, cols[h]].astype(F32)
            delta.append(jnp.sum(prod.T, axis=0, keepdims=True))
            lse.append(lse_ref[h : h + 1, rows])
        keys = []
        g_all = []
        for s in range(5):
            c = b + s
            half = slice(BLK * (c % 2), BLK * (c % 2) + BLK)
            k = tables[c][half, :HD]
            v = tables[c][half, HD:]
            scores = dot(k, q, NT)
            prob_grad = dot(v, do, NT)
            p_parts = []
            g_parts = []
            for h in range(GROUP):
                at = slice(BLK * h, BLK * h + BLK)
                p = jnp.exp(scores[:, at] * scaling - lse[h])
                if s == 4:
                    p = jnp.where(causal, p, 0.0)
                else:
                    m = 3 - s
                    used = picks_ref[0, b, h] == m
                    for t in range(1, 3):
                        used = used | (picks_ref[t, b, h] == m)
                    used = used & (first + b - 1 - m >= 0)
                    p = jnp.where(used, p, 0.0)
                p_parts.append(p.astype(BF))
                g_parts.append((p * (prob_grad[:, at] - delta[h])).astype(BF))
            p_half = jnp.concatenate(p_parts, axis=1)
            g_half = jnp.concatenate(g_parts, axis=1)
            keys.append(k)
            g_all.append(g_half)
            k_part = dot(g_half, q, NN)
            v_part = dot(p_half, do, NN)
            dk[c] = k_part if dk[c] is None else dk[c] + k_part
            dv[c] = v_part if dv[c] is None else dv[c] + v_part
        dq = dot(jnp.concatenate(g_all, axis=0), jnp.concatenate(keys, axis=0), TN)
        for h in range(GROUP):
            aq_ref[rows, cols[h]] = (dq[BLK * h : BLK * h + BLK] * scaling).astype(BF)
    for c in range(6):
        half = slice(BLK * (c % 2), BLK * (c % 2) + BLK)
        sums[c][half, :HD] = (dk[c] * scaling).astype(sums[c].dtype)
        sums[c][half, HD:] = dv[c].astype(sums[c].dtype)


def attention(picks, q, do, o, lse, kv0, kv1, kv2):
    tokens = q.shape[0]
    vm = pl.BlockSpec(memory_space=pltpu.VMEM)
    sm = pl.BlockSpec(memory_space=pltpu.SMEM)
    return pl.pallas_call(
        attention_kernel,
        out_shape=(
            pltpu.VMEM(q.shape, BF),
            pltpu.VMEM((tokens, 2 * HD), F32),
            pltpu.VMEM((tokens, 2 * HD), BF),
            pltpu.VMEM((tokens, 2 * HD), BF),
        ),
        in_specs=[sm] + [vm] * 7,
        out_specs=(vm,) * 4,
        name="attention",
    )(
        picks.transpose(2, 0, 1), q, do, o, lse, placed_in(kv0, pltpu.VMEM),
        placed_in(kv1, pltpu.VMEM), placed_in(kv2, pltpu.VMEM),
    )


def project_kernel(side, q_ref, kv_ref, own_hbm, other_ref, *rest):
    out_hbm, w_ref, out_ref, w_sem, out_sem = rest[-5:]
    zl = lax.axis_index("zl")
    xh = lax.axis_index("xh")
    first = 8 * (xh if side == 0 else 1 - xh)
    loads = []
    for head in range(8):
        for e in range(2):
            k = lax.rem(2 * (head % 2) + e + 4 - zl, 4)
            loads.append(
                pltpu.make_async_copy(
                    own_hbm.at[k, head // 2], w_ref.at[head, e], w_sem.at[head, e]
                )
            )
            loads[-1].start()
    a = jnp.concatenate([q_ref[...], kv_ref[...]], axis=1)
    stores = []
    for head in range(8):
        zh = head // 2
        wide = []
        for e in range(2):
            k = lax.rem(2 * (head % 2) + e + 4 - zl, 4)
            loads[2 * head + e].wait()
            wide += [w_ref[head, e], other_ref[k, zh]]
        w = jnp.concatenate(wide, axis=0)
        out_ref[head] = dot(a, w, NT).astype(BF)
        stores.append(
            pltpu.make_async_copy(out_ref.at[head], out_hbm.at[first + head], out_sem.at[head])
        )
        stores[-1].start()
    for store in stores:
        store.wait()


def placed_in(x, space):
    return pltpu.with_memory_space_constraint(x, space)


def project(side, aq, akv, wc, wo, parts=None):
    hbm = pl.BlockSpec(memory_space=pltpu.HBM)
    vm = pl.BlockSpec(memory_space=pltpu.VMEM)
    rows, cols = wc.shape[2:]
    extra = () if parts is None else (parts,)
    return pl.pallas_call(
        functools.partial(project_kernel, side),
        out_shape=jax.ShapeDtypeStruct((16, 256, 4 * rows), BF),
        in_specs=[vm, vm, hbm, vm] + [hbm] * len(extra),
        out_specs=hbm,
        scratch_shapes=[
            pltpu.VMEM((8, 2, rows, cols), BF),
            pltpu.VMEM((8, 256, 4 * rows), BF),
            pltpu.SemaphoreType.DMA((8, 2)),
            pltpu.SemaphoreType.DMA((8,)),
        ],
        input_output_aliases={4: 0} if extra else {},
    )(placed_in(aq, pltpu.VMEM), placed_in(akv, pltpu.VMEM), wc, placed_in(wo, pltpu.VMEM), *extra)


def total_kernel(in_ref, out_ref):
    swapped = lax.axis_index("core") == 1
    for xh in range(2):
        total = in_ref[8 * xh].astype(F32)
        for h in range(1, 8):
            total = total + in_ref[8 * xh + h].astype(F32)
        for e in range(2):
            at = 256 * e + 128 * xh
            tile = total[:, 128 * e : 128 * e + 128]
            tile = jnp.where(swapped, pltpu.roll(tile, 64, 1), tile)
            out_ref[:, at : at + 128] = tile.astype(BF)


def totalled(parts):
    vm = pl.BlockSpec(memory_space=pltpu.VMEM)
    return pl.pallas_call(
        total_kernel,
        out_shape=jax.ShapeDtypeStruct((parts.shape[1], 512), BF),
        in_specs=[vm],
        out_specs=vm,
        name="total",
    )(placed_in(parts, pltpu.VMEM))


def prepare_kernel(k_ref, v_ref, qw_ref, kw_ref, vw_ref, kv_ref, w_ref):
    kv_ref[:, :HD] = k_ref[...]
    kv_ref[:, HD:] = v_ref[...]
    w_ref[:, : GROUP * HD] = qw_ref[...]
    w_ref[:, GROUP * HD : GROUP * HD + HD] = kw_ref[...]
    w_ref[:, GROUP * HD + HD :] = vw_ref[...]


def prepared(keys, values, qw, kw, vw):
    vm = pl.BlockSpec(memory_space=pltpu.VMEM)
    return pl.pallas_call(
        prepare_kernel,
        out_shape=(
            pltpu.VMEM((keys.shape[0], 2 * HD), BF),
            pltpu.VMEM((qw.shape[0], qw.shape[1] + 2 * HD), BF),
        ),
        in_specs=[vm] * 5,
        out_specs=(vm, vm),
        name="prepare",
    )(keys, values, qw, kw, vw)


def per_device(
    queries, key_rows, value_rows, attn_out, out_grad, log_sums, block_picks,
    query_weight, key_weight, value_weight,
):
    kv0, weight = prepared(key_rows, value_rows, query_weight, key_weight, value_weight)
    kv1 = passed_along(kv0, CTX, 1)
    kv2 = passed_along(kv0, CTX, 2)
    w0 = lax.all_gather(weight, "zh")
    w1 = shifted(w0, Z, -1)
    w3 = shifted(w0, Z, 1)
    w2 = lax.ppermute(w0, Z, [((z + 2 if z % 2 == 0 else z - 2) % 16, z) for z in range(16)])
    aq, own, ret1, ret2 = attention(
        block_picks, queries, out_grad, attn_out, log_sums, kv0, kv1, kv2
    )
    back1 = passed_along(ret1, CTX, -1)
    back2 = passed_along(ret2, CTX, -2)
    aq_far = shifted(aq, "xh", 1)
    wc = jnp.stack([w0, w1, w2, w3])
    wo = shifted(wc, "core", 1)
    akv = (own + back1.astype(F32) + back2.astype(F32)).astype(BF)
    akv_far = shifted(akv, "xh", 1)
    parts = project(0, aq, akv, wc, wo)
    parts = project(1, aq_far, akv_far, wc, wo, parts)
    parts = lax.all_to_all(parts, ("xh", "xl", "y"), 0, 0)
    return totalled(parts)


def solution(mesh):
    wide = Mesh(
        mesh.devices.reshape(4, 4, 2, 2, 2, 4), ("zh", "zl", "xh", "core", "xl", "y")
    )
    both = P(CTX, HEAD)
    placed = (both,) * 5 + (P(HEAD, CTX), P(CTX, HEAD, None)) + (both,) * 3
    return jax.shard_map(
        per_device, mesh=wide, in_specs=placed, out_specs=both, check_vma=False
    )
```
